32 devices in a mesh: scan: 16 (over z, x, core), dict: 2 (over y).
Axes of the slice: x: 2, y: 2, z: 4, core: 2. Of those that a mesh axis runs over, the one named last changes fastest.
Arguments:
- patterns: bfloat16 [3600, 16384], P(None, 'scan'), may hold values from -210 to 210
- dictionary: bfloat16 [3600, 8192], P(None, ('scan', 'dict')), may hold values from -70 to 70
- orientation_quats: bfloat16 [4, 8192], P(None, ('scan', 'dict')), may hold values from -1 to 1
- phase_id: int32 [8192], P(('scan', 'dict')), may hold values from 0 to 2, as said below
- valid_count: int32 [32], P(('scan', 'dict')), may hold values from 1 to 256
Outputs:
- mean_quat: float32 [4, 16384], P(None, 'scan')
- phase_prob: float32 [3, 16384], P(None, 'scan')
The draws below stay inside these ranges and needn't reach their ends.
Inputs may be any that keep to these rules, and one draw needn't show every extreme that they name: `phase_id`: constant within each tile of 256 slots.
All inputs are finite; a program needn't handle non-finite values.
Results may differ from the reference program's by a relative error of at most 0.0029.
Values may be sent and summed in bfloat16 or wider, within the bound.
A program may use at most 128 MiB of HBM per device.

```python
import math
import jax
import jax.numpy as jnp
from jax import lax

PIX = 3600
TILE = 256
REACH = 3
PAT_DEV = 1024
PATTERNS = 16384
ORI = 8192
N_SCAN = 16
N_DICT = 2


def tile_bases(key):
    tiles = ORI // TILE
    base_key = jax.random.fold_in(key, 107)
    bases = jnp.clip(jax.random.normal(base_key, (5, tiles, PIX), jnp.float32), -2.5, 2.5)
    phases = jax.random.uniform(jax.random.fold_in(key, 109), (2, tiles), jnp.float32, 0.0, 2.0 * math.pi)
    return (bases, phases)


def dictionary_columns(key, columns):
    base = jax.random.fold_in(key, 101)
    bases, phases = tile_bases(key)
    tile = columns // TILE
    slot = (columns % TILE).astype(jnp.float32)
    first_angle = 2.0 * math.pi / TILE * slot + phases[0][tile]
    second_angle = 4.0 * math.pi / TILE * slot + phases[1][tile]

    def one_column(column):
        column_key = jax.random.fold_in(base, column)
        first_key, second_key = jax.random.split(column_key)
        values = jnp.clip(jax.random.normal(first_key, (PIX,), jnp.float32), -2.5, 2.5)
        return (values, jax.random.uniform(second_key, (), jnp.float32, -1.0, 1.0))
    noise, offset = jax.vmap(one_column)(columns)
    values = bases[0][tile]
    values = values + jnp.cos(first_angle)[:, None] * bases[1][tile]
    values = values + jnp.sin(first_angle)[:, None] * bases[2][tile]
    values = values + jnp.cos(second_angle)[:, None] * bases[3][tile]
    values = values + jnp.sin(second_angle)[:, None] * bases[4][tile]
    values = values + 0.6 * noise
    values = values * (1.0 / 1.85) + offset[:, None]
    return values.T


def tile_valid(key):
    tiles = ORI // TILE
    first_key, second_key, third_key = jax.random.split(jax.random.fold_in(key, 201), 3)
    trimmed = jax.random.randint(first_key, (tiles,), 0, TILE)
    filled = jax.random.randint(second_key, (tiles,), 0, 4) == 0
    chosen = jax.random.randint(third_key, (), 0, tiles)
    filled = filled | (jnp.arange(tiles) == chosen)
    return jnp.where(filled, TILE, TILE - trimmed).astype(jnp.int32)


def draw_valid_count(key, part):
    return tile_valid(key)


def draw_phase_id(key, part):
    per_tile = jax.random.randint(jax.random.fold_in(key, 301), (ORI // TILE,), 0, 3)
    return jnp.repeat(per_tile, TILE).astype(jnp.int32)


def draw_dictionary(key, part):
    values = dictionary_columns(key, jnp.arange(ORI, dtype=jnp.int32))
    return values.astype(jnp.bfloat16)


def draw_patterns(key, part):
    scan_rows = PATTERNS // PAT_DEV
    row_tiles = ORI // (TILE * scan_rows)
    keys = jax.random.split(jax.random.fold_in(key, 401), 10)
    block = jnp.arange(PATTERNS, dtype=jnp.int32) // PAT_DEV
    valid = tile_valid(key)
    first_row = (block + jax.random.randint(keys[0], (PATTERNS,), -REACH, REACH + 1)) % scan_rows
    first_tile = first_row * row_tiles + jax.random.randint(keys[1], (PATTERNS,), 0, row_tiles)
    first_slot = jax.random.randint(keys[2], (PATTERNS,), 0, valid[first_tile])
    first_column = first_tile * TILE + first_slot
    second_row = (block + jax.random.randint(keys[3], (PATTERNS,), -REACH, REACH + 1)) % scan_rows
    second_tile = second_row * row_tiles + jax.random.randint(keys[4], (PATTERNS,), 0, row_tiles)
    second_column = second_tile * TILE + jax.random.randint(keys[5], (PATTERNS,), 0, TILE)
    first_weight = jax.random.uniform(keys[6], (PATTERNS,), jnp.float32, 0.5, 1.0)
    second_weight = jax.random.uniform(keys[7], (PATTERNS,), jnp.float32, 0.5, 1.0)
    noise = jnp.clip(jax.random.normal(keys[8], (PIX, PATTERNS), jnp.float32), -6.0, 6.0)
    offsets = jax.random.uniform(keys[9], (PATTERNS,), jnp.float32, -2.0, 2.0)
    values = first_weight[None, :] * dictionary_columns(key, first_column)
    values = values + second_weight[None, :] * dictionary_columns(key, second_column)
    values = values + noise
    values = values + offsets[None, :]
    return values.astype(jnp.bfloat16)


def shard_levels(own_key, dims, cuts, low, high):
    level = 1.0
    for axis_at, blocks in cuts:
        heights = jax.random.uniform(jax.random.fold_in(jax.random.fold_in(own_key, 6), axis_at), (blocks,), jnp.float32, low / len(cuts), high / len(cuts))
        level = level * jnp.repeat(jnp.exp(heights), dims[axis_at] // blocks).reshape((-1,) + (1,) * (len(dims) - 1 - axis_at))
    return level


def setup_inputs(seed: int = 0) -> dict:
    key_of = jax.random.split(jax.random.key(seed), 6)
    return {
        "patterns": draw_patterns(jax.random.fold_in(key_of[5], 71), 0),
        "dictionary": draw_dictionary(jax.random.fold_in(key_of[5], 71), 0),
        "orientation_quats": jnp.clip(jax.random.uniform(key_of[2], (4, ORI), jnp.float32, -1.0, 1.0) * shard_levels(key_of[2], (4, ORI), ((1, 32),), -0.4, 0.0), -1.0, 1.0).astype(jnp.bfloat16),
        "phase_id": draw_phase_id(jax.random.fold_in(key_of[5], 71), 0),
        "valid_count": draw_valid_count(jax.random.fold_in(key_of[5], 71), 0),
    }


EPS = 1e-05
SHARPNESS = 40.0

def unit_columns(values):
    widened = values.astype(jnp.float32)
    centred = widened - lax.optimization_barrier(jnp.mean(widened, axis=0, keepdims=True))
    mean_square = lax.optimization_barrier(jnp.mean(centred * centred, axis=0, keepdims=True))
    return (centred * lax.rsqrt((mean_square + EPS) * values.shape[0])).astype(jnp.bfloat16)

def contribute(unit_tile, table_rows, unit_pats):
    cosine = jnp.dot(unit_tile.T, unit_pats, preferred_element_type=jnp.float32)
    weights = jnp.exp(SHARPNESS * (cosine - 1.0)).astype(jnp.bfloat16)
    return jnp.dot(table_rows, weights, preferred_element_type=jnp.float32)

def reference(patterns, dictionary, orientation_quats, phase_id, valid_count):
    row_length = N_DICT * TILE
    dict_rows = jnp.moveaxis(dictionary.reshape(PIX, N_SCAN, row_length), 1, 0)
    unit_rows = lax.map(unit_columns, dict_rows)
    live_slots = (jnp.arange(ORI) % TILE < jnp.repeat(valid_count, TILE)).astype(jnp.float32)
    phase_rows = (phase_id[None, :] == jnp.arange(3)[:, None]).astype(jnp.float32)
    tile_table = jnp.concatenate([orientation_quats.astype(jnp.float32), phase_rows, jnp.ones((1, ORI), jnp.float32)], 0)
    tile_table = (tile_table * live_slots[None, :]).astype(jnp.bfloat16)
    table_blocks = jnp.moveaxis(tile_table.reshape(8, N_SCAN, row_length), 1, 0)
    pattern_blocks = jnp.moveaxis(patterns.reshape(PIX, N_SCAN, PAT_DEV), 1, 0)

    def one_block(block_index):
        unit_pats = unit_columns(pattern_blocks[block_index])
        running = jnp.zeros((8, PAT_DEV), jnp.float32)
        for row_offset in range(-REACH, REACH + 1):
            source = (block_index + row_offset) % N_SCAN
            running = running + contribute(unit_rows[source], table_blocks[source], unit_pats)
        return running
    totals = lax.map(one_block, jnp.arange(N_SCAN, dtype=jnp.int32))
    totals = jnp.moveaxis(totals, 0, 1).reshape(8, PATTERNS)
    denominator = totals[7:8]
    return (totals[0:4] / denominator, totals[4:7] / denominator)
```

```python
import functools

import jax
import jax.numpy as jnp
from jax import lax
from jax.experimental import pallas as pl
from jax.experimental.pallas import tpu as pltpu
from jax.sharding import PartitionSpec as P

REACH = 3
SLOTS = 2 * REACH + 1
EPS = 1e-05
SHARPNESS = 40.0
LAYER = 4


def chunk_count(pixels):
    for count in (5, 9, 3, 15, 2, 4, 8):
        if pixels % (16 * count) == 0:
            return count
    return 1


def kernel(
    n, n_dict, chunks, tile_ref, pats_ref, quats_ref, phase_ref, valid_ref,
    quat_out, prob_out,
    buf, pats, meta, acc, sums, totals,
    ssem, rsem, meta_ssem, meta_rsem, load_sem, sum_ssem, sum_rsem,
):
    pixels, slots = tile_ref.shape
    rows = pixels // chunks
    own = REACH
    me = lax.axis_index("scan")
    my_dict = lax.axis_index("dict")
    j = lax.rem(me, LAYER)
    sign = jnp.where(j < 2, 1, -1)
    role = jnp.where((j == 0) | (j == LAYER - 1), 0, 1)
    rho = 1 - 2 * role

    def at(offset):
        return lax.rem(me + offset + n, n)

    def chunk(i):
        return pl.ds(pl.multiple_of(i * rows, 16), rows)

    barrier = pltpu.get_barrier_semaphore()
    for offset in (-4, -3, -2, -1, 1, 2, 3, 4):
        pl.semaphore_signal(barrier, inc=1, device_id={"scan": at(offset)})
    for d in range(1, n_dict):
        pl.semaphore_signal(
            barrier, inc=1, device_id={"dict": lax.rem(my_dict + d, n_dict)}
        )
    load_pats = pltpu.make_async_copy(pats_ref, pats, load_sem.at[0])
    load_tile = pltpu.make_async_copy(tile_ref, buf.at[own], load_sem.at[1])
    load_tile.start()
    load_pats.start()
    pl.semaphore_wait(barrier, 8 + n_dict - 1)

    partner = rho * sign
    core_own = (0, None, partner, -rho)
    x_own = (1, None, 2 * sign, 2)
    z_own = (2, None, -3 * partner, 3 * rho)
    relay = (3, 2 + role, (4 - 2 * role) * sign, role - 2)
    core_mid = (4, 2, partner, 2 - rho)
    core_far = (5, -2, partner, -3)
    core_near = (6, -1, partner, -2)

    def send(flow, i):
        number, source, offset, slot = flow
        src = tile_ref.at[chunk(i)] if source is None else buf.at[source + own, chunk(i)]
        return pltpu.make_async_remote_copy(
            src_ref=src,
            dst_ref=buf.at[slot + own, chunk(i)],
            send_sem=ssem.at[number, i],
            recv_sem=rsem.at[slot + own, i],
            device_id={"scan": at(offset)},
        )

    def arrive(slot, i):
        pltpu.make_async_copy(
            tile_ref.at[chunk(i)], buf.at[slot + own, chunk(i)], rsem.at[slot + own, i]
        ).wait()

    @pl.loop(0, chunks)
    def _(i):
        send(x_own, i).start()
        send(z_own, i).start()
        send(core_own, i).start()

    load_tile.wait()

    def column_stats(ref, pieces):
        size = pixels // pieces
        width = ref.shape[-1]

        def piece(i):
            return ref[pl.ds(pl.multiple_of(i * size, 16), size), :].astype(jnp.float32)

        zero = jnp.zeros((1, width), jnp.float32)
        mean = lax.fori_loop(
            0, pieces, lambda i, s: s + jnp.sum(piece(i), axis=0, keepdims=True), zero
        ) / pixels

        def squares(i, s):
            c = piece(i) - mean
            return s + jnp.sum(c * c, axis=0, keepdims=True)

        mean_square = lax.fori_loop(0, pieces, squares, zero) / pixels
        return mean, lax.rsqrt((mean_square + EPS) * pixels)

    mean, scale = column_stats(buf.at[own], 15)
    live = (
        lax.broadcasted_iota(jnp.int32, (1, slots), 1) < valid_ref[0]
    ).astype(jnp.float32)
    phase = phase_ref[...]
    meta[own, 0:4, :] = quats_ref[...].astype(jnp.float32) * live
    for p in range(3):
        meta[own, 4 + p : 5 + p, :] = (phase == p).astype(jnp.float32) * live
    meta[own, 7:8, :] = live
    meta[own, 8:9, :] = mean
    meta[own, 9:10, :] = scale
    meta[own, 10:16, :] = jnp.zeros((6, slots), jnp.float32)

    def send_meta(index, offset):
        there = jnp.where(lax.rem(at(offset), LAYER) < 2, 1, -1)
        slot = own - there * offset
        return pltpu.make_async_remote_copy(
            src_ref=meta.at[own],
            dst_ref=meta.at[slot],
            send_sem=meta_ssem.at[index],
            recv_sem=meta_rsem.at[slot],
            device_id={"scan": at(offset)},
        )

    offsets = (-3, -2, -1, 1, 2, 3)
    for index, offset in enumerate(offsets):
        send_meta(index, offset).start()

    load_pats.wait()
    p_mean, p_scale = column_stats(pats, 25)

    @pl.loop(0, 25)
    def _(i):
        part = pl.ds(pl.multiple_of(i * (pixels // 25), 16), pixels // 25)
        pats[part, :] = ((pats[part, :].astype(jnp.float32) - p_mean) * p_scale).astype(
            jnp.bfloat16
        )

    totals[...] = jnp.zeros_like(totals)

    def meta_arrive(slot):
        pltpu.make_async_copy(
            meta.at[own], meta.at[slot + own], meta_rsem.at[slot + own]
        ).wait()

    def accumulate(which, slot, i):
        m = meta[slot + own, 8:9, :]
        s = meta[slot + own, 9:10, :]
        unit = ((buf[slot + own, chunk(i), :].astype(jnp.float32) - m) * s).astype(
            jnp.bfloat16
        )
        product = lax.dot_general(
            unit, pats[chunk(i), :], (((0,), (0,)), ((), ())),
            preferred_element_type=jnp.float32,
        )

        @pl.when(i == 0)
        def _():
            acc[which] = product

        @pl.when(i > 0)
        def _():
            acc[which] += product

    def finish(which, slot):
        weights = jnp.exp(SHARPNESS * (acc[which] - 1.0)).astype(jnp.bfloat16)
        table = meta[slot + own, 0:8, :].astype(jnp.bfloat16)
        totals[...] += jnp.dot(table, weights, preferred_element_type=jnp.float32)

    meta_arrive(rho)

    @pl.loop(0, chunks)
    def _(i):
        arrive(rho, i)
        accumulate(0, 0, i)
        accumulate(1, rho, i)

    finish(0, 0)
    finish(1, rho)

    z_slot = -3 * rho
    meta_arrive(2)
    meta_arrive(z_slot)

    @pl.loop(0, chunks)
    def _(i):
        arrive(2, i)
        arrive(z_slot, i)
        send(relay, i).start()
        send(core_mid, i).start()
        accumulate(0, 2, i)
        accumulate(1, z_slot, i)

    finish(0, 2)
    finish(1, z_slot)

    mid_slot = 2 + rho
    meta_arrive(mid_slot)

    @pl.loop(0, chunks)
    def _(i):
        arrive(mid_slot, i)
        accumulate(0, mid_slot, i)

    finish(0, mid_slot)

    far_slot = -2 - role
    near_slot = -1 - role
    meta_arrive(far_slot)
    meta_arrive(near_slot)

    @pl.loop(0, chunks)
    def _(i):
        arrive(far_slot, i)

        @pl.when(role == 0)
        def _():
            send(core_far, i).start()

        arrive(near_slot, i)

        @pl.when(role == 0)
        def _():
            send(core_near, i).start()

        accumulate(0, far_slot, i)
        accumulate(1, near_slot, i)

    finish(0, far_slot)
    finish(1, near_slot)

    sums[my_dict] = totals[...]

    def send_sum(d):
        return pltpu.make_async_remote_copy(
            src_ref=totals,
            dst_ref=sums.at[my_dict],
            send_sem=sum_ssem.at[d],
            recv_sem=sum_rsem.at[my_dict],
            device_id={"dict": lax.rem(my_dict + d, n_dict)},
        )

    for d in range(1, n_dict):
        send_sum(d).start()
    for d in range(1, n_dict):
        source = lax.rem(my_dict + d, n_dict)
        pltpu.make_async_copy(totals, sums.at[source], sum_rsem.at[source]).wait()
    whole = sums[0]
    for d in range(1, n_dict):
        whole = whole + sums[d]
    denominator = whole[7:8]
    quat_out[...] = whole[0:4] / denominator
    prob_out[...] = whole[4:7] / denominator

    @pl.loop(0, chunks)
    def _(i):
        for flow in (x_own, z_own, core_own, relay, core_mid):
            send(flow, i).wait_send()

        @pl.when(role == 0)
        def _():
            send(core_far, i).wait_send()
            send(core_near, i).wait_send()

    for index, offset in enumerate(offsets):
        send_meta(index, offset).wait_send()
    for d in range(1, n_dict):
        send_sum(d).wait_send()


def solution(mesh):
    n = mesh.shape["scan"]
    n_dict = mesh.shape["dict"]

    def per_device(patterns, dictionary, orientation_quats, phase_id, valid_count):
        pixels, slots = dictionary.shape
        count = patterns.shape[1]
        chunks = chunk_count(pixels)
        vmem = pl.BlockSpec(memory_space=pltpu.VMEM)
        hbm = pl.BlockSpec(memory_space=pltpu.HBM)
        return pl.pallas_call(
            functools.partial(kernel, n, n_dict, chunks),
            out_shape=(
                jax.ShapeDtypeStruct((4, count), jnp.float32),
                jax.ShapeDtypeStruct((3, count), jnp.float32),
            ),
            in_specs=[hbm, hbm, vmem, vmem, pl.BlockSpec(memory_space=pltpu.SMEM)],
            out_specs=(vmem, vmem),
            scratch_shapes=[
                pltpu.VMEM((SLOTS, pixels, slots), jnp.bfloat16),
                pltpu.VMEM((pixels, count), jnp.bfloat16),
                pltpu.VMEM((SLOTS, 16, slots), jnp.float32),
                pltpu.VMEM((2, slots, count), jnp.float32),
                pltpu.VMEM((n_dict, 8, count), jnp.float32),
                pltpu.VMEM((8, count), jnp.float32),
                pltpu.SemaphoreType.DMA((7, chunks)),
                pltpu.SemaphoreType.DMA((SLOTS, chunks)),
                pltpu.SemaphoreType.DMA((6,)),
                pltpu.SemaphoreType.DMA((SLOTS,)),
                pltpu.SemaphoreType.DMA((2,)),
                pltpu.SemaphoreType.DMA((n_dict,)),
                pltpu.SemaphoreType.DMA((n_dict,)),
            ],
            compiler_params=pltpu.CompilerParams(
                collective_id=0, has_side_effects=True, vmem_limit_bytes=48 * 2**20
            ),
        )(dictionary, patterns, orientation_quats, phase_id.reshape(1, slots), valid_count)

    in_specs = (
        P(None, "scan"),
        P(None, ("scan", "dict")),
        P(None, ("scan", "dict")),
        P(("scan", "dict")),
        P(("scan", "dict")),
    )
    out_specs = (P(None, "scan"), P(None, "scan"))
    return jax.shard_map(
        per_device, mesh=mesh, in_specs=in_specs, out_specs=out_specs, check_vma=False
    )
```

```python
import functools

import jax
import jax.numpy as jnp
from jax import lax
from jax.experimental import pallas as pl
from jax.experimental.pallas import tpu as pltpu
from jax.sharding import PartitionSpec as P

REACH = 3
SLOTS = 2 * REACH + 1
EPS = 1e-05
SHARPNESS = 40.0
LAYER = 4


def chunk_count(pixels):
    for count in (5, 9, 3, 15, 2, 4, 8):
        if pixels % (16 * count) == 0:
            return count
    return 1


def kernel(
    n, n_dict, chunks, tile_ref, pats_ref, quats_ref, phase_ref, valid_ref,
    quat_out, prob_out,
    buf, pats, meta, acc, sums, totals,
    ssem, rsem, meta_ssem, meta_rsem, load_sem, sum_ssem, sum_rsem,
):
    pixels, slots = tile_ref.shape
    rows = pixels // chunks
    own = REACH
    me = lax.axis_index("scan")
    my_dict = lax.axis_index("dict")
    j = lax.rem(me, LAYER)
    sign = jnp.where(j < 2, 1, -1)
    role = jnp.where((j == 0) | (j == LAYER - 1), 0, 1)
    rho = 1 - 2 * role

    def at(offset):
        return lax.rem(me + offset + n, n)

    def chunk(i):
        return pl.ds(pl.multiple_of(i * rows, 16), rows)

    barrier = pltpu.get_barrier_semaphore()
    for offset in (-4, -3, -2, -1, 1, 2, 3, 4):
        pl.semaphore_signal(barrier, inc=1, device_id={"scan": at(offset)})
    for d in range(1, n_dict):
        pl.semaphore_signal(
            barrier, inc=1, device_id={"dict": lax.rem(my_dict + d, n_dict)}
        )
    load_pats = pltpu.make_async_copy(pats_ref, pats, load_sem.at[0])
    load_tile = pltpu.make_async_copy(tile_ref, buf.at[own], load_sem.at[1])
    load_tile.start()
    load_pats.start()
    pl.semaphore_wait(barrier, 8 + n_dict - 1)

    partner = rho * sign
    core_own = (0, None, partner, -rho)
    x_own = (1, None, 2 * sign, 2)
    z_own = (2, None, -3 * partner, 3 * rho)
    relay = (3, 2 + role, (4 - 2 * role) * sign, role - 2)
    core_mid = (4, 2, partner, 2 - rho)
    core_far = (5, -2, partner, -3)
    core_near = (6, -1, partner, -2)

    def send(flow, i):
        number, source, offset, slot = flow
        src = tile_ref.at[chunk(i)] if source is None else buf.at[source + own, chunk(i)]
        return pltpu.make_async_remote_copy(
            src_ref=src,
            dst_ref=buf.at[slot + own, chunk(i)],
            send_sem=ssem.at[number, i],
            recv_sem=rsem.at[slot + own, i],
            device_id={"scan": at(offset)},
        )

    def arrive(slot, i):
        pltpu.make_async_copy(
            tile_ref.at[chunk(i)], buf.at[slot + own, chunk(i)], rsem.at[slot + own, i]
        ).wait()

    @pl.loop(0, chunks)
    def _(i):
        send(x_own, i).start()
        send(z_own, i).start()
        send(core_own, i).start()

    load_tile.wait()

    def column_stats(ref, pieces):
        size = pixels // pieces
        width = ref.shape[-1]

        def piece(i):
            return ref[pl.ds(pl.multiple_of(i * size, 16), size), :].astype(jnp.float32)

        zero = jnp.zeros((1, width), jnp.float32)
        mean = lax.fori_loop(
            0, pieces, lambda i, s: s + jnp.sum(piece(i), axis=0, keepdims=True), zero
        ) / pixels

        def squares(i, s):
            c = piece(i) - mean
            return s + jnp.sum(c * c, axis=0, keepdims=True)

        mean_square = lax.fori_loop(0, pieces, squares, zero) / pixels
        return mean, lax.rsqrt((mean_square + EPS) * pixels)

    mean, scale = column_stats(buf.at[own], 15)
    live = (
        lax.broadcasted_iota(jnp.int32, (1, slots), 1) < valid_ref[0]
    ).astype(jnp.float32)
    phase = phase_ref[...]
    meta[own, 0:4, :] = quats_ref[...].astype(jnp.float32) * live
    for p in range(3):
        meta[own, 4 + p : 5 + p, :] = (phase == p).astype(jnp.float32) * live
    meta[own, 7:8, :] = live
    meta[own, 8:9, :] = mean
    meta[own, 9:10, :] = scale
    meta[own, 10:16, :] = jnp.zeros((6, slots), jnp.float32)

    def send_meta(index, offset):
        there = jnp.where(lax.rem(at(offset), LAYER) < 2, 1, -1)
        slot = own - there * offset
        return pltpu.make_async_remote_copy(
            src_ref=meta.at[own],
            dst_ref=meta.at[slot],
            send_sem=meta_ssem.at[index],
            recv_sem=meta_rsem.at[slot],
            device_id={"scan": at(offset)},
        )

    offsets = (-3, -2, -1, 1, 2, 3)
    for index, offset in enumerate(offsets):
        send_meta(index, offset).start()

    load_pats.wait()
    p_mean, p_scale = column_stats(pats, 25)

    @pl.loop(0, 25)
    def _(i):
        part = pl.ds(pl.multiple_of(i * (pixels // 25), 16), pixels // 25)
        pats[part, :] = ((pats[part, :].astype(jnp.float32) - p_mean) * p_scale).astype(
            jnp.bfloat16
        )

    totals[...] = jnp.zeros_like(totals)

    def meta_arrive(slot):
        pltpu.make_async_copy(
            meta.at[own], meta.at[slot + own], meta_rsem.at[slot + own]
        ).wait()

    def accumulate(which, slot, i):
        m = meta[slot + own, 8:9, :]
        s = meta[slot + own, 9:10, :]
        unit = ((buf[slot + own, chunk(i), :].astype(jnp.float32) - m) * s).astype(
            jnp.bfloat16
        )
        product = lax.dot_general(
            unit, pats[chunk(i), :], (((0,), (0,)), ((), ())),
            preferred_element_type=jnp.float32,
        )

        @pl.when(i == 0)
        def _():
            acc[which] = product

        @pl.when(i > 0)
        def _():
            acc[which] += product

    def finish(which, slot):
        weights = jnp.exp(SHARPNESS * (acc[which] - 1.0)).astype(jnp.bfloat16)
        table = meta[slot + own, 0:8, :].astype(jnp.bfloat16)
        totals[...] += jnp.dot(table, weights, preferred_element_type=jnp.float32)

    meta_arrive(rho)

    @pl.loop(0, chunks)
    def _(i):
        arrive(rho, i)
        accumulate(0, 0, i)
        accumulate(1, rho, i)

    finish(0, 0)
    finish(1, rho)

    z_slot = -3 * rho

    @pl.loop(0, chunks)
    def _(i):
        arrive(2, i)
        arrive(z_slot, i)
        send(relay, i).start()
        send(core_mid, i).start()

    meta_arrive(2)
    meta_arrive(z_slot)

    @pl.loop(0, chunks)
    def _(i):
        accumulate(0, 2, i)
        accumulate(1, z_slot, i)

    finish(0, 2)
    finish(1, z_slot)

    mid_slot = 2 + rho
    meta_arrive(mid_slot)

    @pl.loop(0, chunks)
    def _(i):
        arrive(mid_slot, i)
        accumulate(0, mid_slot, i)

    finish(0, mid_slot)

    far_slot = -2 - role
    near_slot = -1 - role
    meta_arrive(far_slot)
    meta_arrive(near_slot)

    @pl.loop(0, chunks)
    def _(i):
        arrive(far_slot, i)

        @pl.when(role == 0)
        def _():
            send(core_far, i).start()

        arrive(near_slot, i)

        @pl.when(role == 0)
        def _():
            send(core_near, i).start()

        accumulate(0, far_slot, i)
        accumulate(1, near_slot, i)

    finish(0, far_slot)
    finish(1, near_slot)

    sums[my_dict] = totals[...]

    def send_sum(d):
        return pltpu.make_async_remote_copy(
            src_ref=totals,
            dst_ref=sums.at[my_dict],
            send_sem=sum_ssem.at[d],
            recv_sem=sum_rsem.at[my_dict],
            device_id={"dict": lax.rem(my_dict + d, n_dict)},
        )

    for d in range(1, n_dict):
        send_sum(d).start()
    for d in range(1, n_dict):
        source = lax.rem(my_dict + d, n_dict)
        pltpu.make_async_copy(totals, sums.at[source], sum_rsem.at[source]).wait()
    whole = sums[0]
    for d in range(1, n_dict):
        whole = whole + sums[d]
    denominator = whole[7:8]
    quat_out[...] = whole[0:4] / denominator
    prob_out[...] = whole[4:7] / denominator

    @pl.loop(0, chunks)
    def _(i):
        for flow in (x_own, z_own, core_own, relay, core_mid):
            send(flow, i).wait_send()

        @pl.when(role == 0)
        def _():
            send(core_far, i).wait_send()
            send(core_near, i).wait_send()

    for index, offset in enumerate(offsets):
        send_meta(index, offset).wait_send()
    for d in range(1, n_dict):
        send_sum(d).wait_send()


def solution(mesh):
    n = mesh.shape["scan"]
    n_dict = mesh.shape["dict"]

    def per_device(patterns, dictionary, orientation_quats, phase_id, valid_count):
        pixels, slots = dictionary.shape
        count = patterns.shape[1]
        chunks = chunk_count(pixels)
        vmem = pl.BlockSpec(memory_space=pltpu.VMEM)
        hbm = pl.BlockSpec(memory_space=pltpu.HBM)
        return pl.pallas_call(
            functools.partial(kernel, n, n_dict, chunks),
            out_shape=(
                jax.ShapeDtypeStruct((4, count), jnp.float32),
                jax.ShapeDtypeStruct((3, count), jnp.float32),
            ),
            in_specs=[hbm, hbm, vmem, vmem, pl.BlockSpec(memory_space=pltpu.SMEM)],
            out_specs=(vmem, vmem),
            scratch_shapes=[
                pltpu.VMEM((SLOTS, pixels, slots), jnp.bfloat16),
                pltpu.VMEM((pixels, count), jnp.bfloat16),
                pltpu.VMEM((SLOTS, 16, slots), jnp.float32),
                pltpu.VMEM((2, slots, count), jnp.float32),
                pltpu.VMEM((n_dict, 8, count), jnp.float32),
                pltpu.VMEM((8, count), jnp.float32),
                pltpu.SemaphoreType.DMA((7, chunks)),
                pltpu.SemaphoreType.DMA((SLOTS, chunks)),
                pltpu.SemaphoreType.DMA((6,)),
                pltpu.SemaphoreType.DMA((SLOTS,)),
                pltpu.SemaphoreType.DMA((2,)),
                pltpu.SemaphoreType.DMA((n_dict,)),
                pltpu.SemaphoreType.DMA((n_dict,)),
            ],
            compiler_params=pltpu.CompilerParams(
                collective_id=0, has_side_effects=True, vmem_limit_bytes=48 * 2**20
            ),
        )(dictionary, patterns, orientation_quats, phase_id.reshape(1, slots), valid_count)

    in_specs = (
        P(None, "scan"),
        P(None, ("scan", "dict")),
        P(None, ("scan", "dict")),
        P(("scan", "dict")),
        P(("scan", "dict")),
    )
    out_specs = (P(None, "scan"), P(None, "scan"))
    return jax.shard_map(
        per_device, mesh=mesh, in_specs=in_specs, out_specs=out_specs, check_vma=False
    )
```
